512 devices in a mesh: section: 2 (over core), dp: 16 (over z), mp: 16 (over y, x).
Axes of the slice: x: 4, y: 4, z: 16, core: 2. Of those that a mesh axis runs over, the one named last changes fastest.
Arguments:
- events: bfloat16 [512, 1024, 512], P(('section', 'dp', 'mp')), may hold values from -6 to 6
- hist_len: int32 [512], P(('section', 'dp', 'mp')), may hold values from 256 to 1024, as said below
- sess_len: int32 [512, 32], P(('section', 'dp', 'mp')), may hold values from 1 to 64, 1024 in all within a row
- w_uvqk: bfloat16 [512, 2048], P('dp'), may hold values from -0.25 to 0.25
- w_out: bfloat16 [512, 512], P('dp'), may hold values from -0.25 to 0.25
- attn_gain: float32 [512], replicated, may hold values from 0.1 to 1.9
- w_in: bfloat16 [512, 4096], P(None, ('section', 'mp')), may hold values from -2 to 2
- ffn_gain: bfloat16 [1, 4096], P(None, ('section', 'mp')), may hold values from 0.099609375 to 1.8984375
- w_up: bfloat16 [4096, 8192], P('section', 'mp'), may hold values from -0.09375 to 0.09375
- w_down: bfloat16 [8192, 4096], P('mp', 'section'), may hold values from -0.0625 to 0.0625
Outputs:
- pooled: bfloat16 [16384, 512], P(('section', 'dp', 'mp'))
- cross_out: bfloat16 [4096, 4096], P(('section', 'dp', 'mp'))
The draws below stay inside these ranges and needn't reach their ends.
Inputs may be any that keep to these rules, and one draw needn't show every extreme that they name: `hist_len`: some user has all 1024 events valid. `sess_len`: a user's 32 sessions cover all 1024 positions; some session has exactly 64 events.
All inputs are finite; a program needn't handle non-finite values.
Results may differ from the reference program's by a relative error of at most 0.015.
Values may be sent and summed in bfloat16 or wider, within the bound.
A program may use at most 64 MiB of HBM per device.

```python
import math
import jax
import jax.numpy as jnp
import numpy as np
from jax import lax

E = 512
HEADS = 4
DM = 4096
FF = 8192
SESS = 32
MICRO = 4
SESS_MAX = 64
L = 1024
USERS = 512


def draw_hist_len(key, part):
    drawn = jax.random.randint(key, (USERS,), L // 4, L + 1, dtype=jnp.int32)
    return drawn.at[0].set(L).at[1].set(L // 4)


def draw_w_in(key, part):
    key_base, key_col = jax.random.split(jax.random.fold_in(key, 7), 2)
    columns = jnp.arange(DM, dtype=jnp.float32)
    jitter = jax.random.uniform(key_col, (DM,), jnp.float32, 0.0, 1.0)
    col_scale = 10.0 ** ((columns + DM * 0.125 * jitter) / (DM * 1.125))
    base_draw = jnp.clip(jax.random.normal(key_base, (E, DM), jnp.float32), -4.0, 4.0)
    scaled = base_draw * col_scale[None, :] * E ** (-0.5)
    return jnp.clip(scaled, -2.0, 2.0).astype(jnp.bfloat16)


def level_of(own_key, dims, cuts, low, high):
    level = 1.0
    for axis_at, blocks in cuts:
        draws = jax.random.uniform(jax.random.fold_in(jax.random.fold_in(own_key, 6), axis_at), (blocks,), jnp.float32, low / len(cuts), high / len(cuts))
        level = level * jnp.repeat(jnp.exp(draws), dims[axis_at] // blocks).reshape((-1,) + (1,) * (len(dims) - 1 - axis_at))
    return level


def split_up(number_of, total, most, skew):
    loads = [(1 << 20) // math.isqrt(rank ** skew) + 1 for rank in range(2, number_of + 1)]
    spare, given = total - most - (number_of - 1), [1] * (number_of - 1)
    while spare > 0:
        candidates = [i for i in range(number_of - 1) if given[i] < most]
        mass, left = sum([loads[i] for i in candidates]), spare
        for i in candidates:
            more = min(most - given[i], max(1, left * loads[i] // mass), spare)
            given[i] = given[i] + more
            spare = spare - more
    return np.array([most] + given)


def ragged_sizes(rng, number_of, total, bound, skew):
    if number_of == 2:
        one = jax.random.randint(rng, (), max(1, total - bound), min(bound, total - 1) + 1)
        return jnp.stack([one, total - one])
    lengths = jnp.asarray(split_up(number_of, total, bound, skew), jnp.int32)
    twos = (number_of - 1) // 2
    donor, sink = lengths[1:1 + 2 * twos:2], lengths[2:2 + 2 * twos:2]
    margin = jnp.minimum(donor - 1, bound - sink)
    shifted = jax.random.randint(jax.random.fold_in(rng, 1), (twos,), 0, 1 << 20) % (margin + 1)
    lengths = lengths.at[1:1 + 2 * twos:2].set(donor - shifted).at[2:2 + 2 * twos:2].set(sink + shifted)
    return lengths[jax.random.permutation(jax.random.fold_in(rng, 2), number_of)]


def gaussian(key, extent, deviation, bound, cuts=(), kind=jnp.bfloat16):
    entries = jax.random.normal(key, extent, jnp.float32) * deviation
    if len(cuts) > 0:
        entries = level_of(key, extent, cuts, -0.22, 0.18) * entries
    return jnp.clip(entries, min=-bound, max=bound).astype(kind)


def setup_inputs(seed: int = 0) -> dict:
    keys = jax.random.split(jax.random.key(seed), 11)
    return {
        "events": gaussian(keys[0], (USERS, L, E), 1.0, 6.0, ((0, 512),)),
        "hist_len": draw_hist_len(jax.random.fold_in(keys[10], 71), 0),
        "sess_len": jax.vmap(lambda own: ragged_sizes(own, SESS, SESS * 32, SESS_MAX, 1))(jax.random.split(keys[2], USERS)).reshape((USERS, SESS)).astype(jnp.int32),
        "w_uvqk": gaussian(keys[3], (E, 4 * E), E ** -0.5, 0.25, ((0, 16),)),
        "w_out": gaussian(keys[4], (E, E), E ** -0.5, 0.25, ((0, 16),)),
        "attn_gain": jnp.clip(1.0 + 0.18 * jax.random.normal(keys[5], (E,), jnp.float32), 0.1, 1.9),
        "w_in": draw_w_in(jax.random.fold_in(keys[10], 71), 0),
        "ffn_gain": jnp.clip(1.0 + 0.18 * jax.random.normal(keys[7], (1, DM), jnp.float32), 0.099609375, 1.8984375).astype(jnp.bfloat16),
        "w_up": gaussian(keys[8], (DM, FF), DM ** -0.5, 0.09375, ((0, 2), (1, 16))),
        "w_down": gaussian(keys[9], (FF, DM), FF ** -0.5, 0.0625, ((0, 16), (1, 2))),
    }


EPSILON = 1e-06

def encode_user(tokens, valid_len, w_uvqk, w_out, norm_gain):
    length, model_width = tokens.shape
    head_dim = model_width // HEADS
    projected = jnp.dot(tokens, w_uvqk, preferred_element_type=jnp.float32)
    activated = jax.nn.silu(projected)
    gate_part = activated[:, :model_width]
    values = activated[:, model_width:2 * model_width].astype(jnp.bfloat16)
    queries = activated[:, 2 * model_width:3 * model_width].astype(jnp.bfloat16)
    key_vecs = activated[:, 3 * model_width:].astype(jnp.bfloat16)
    values, queries, key_vecs = lax.optimization_barrier((values, queries, key_vecs))
    key_heads = key_vecs.reshape(length, HEADS, head_dim).astype(jnp.float32)
    value_heads = values.reshape(length, HEADS, head_dim).astype(jnp.float32)
    block_rows = min(length, 512)
    columns = jnp.arange(length, dtype=jnp.int32)
    outputs = []
    for block_index in range(length // block_rows):
        query_heads = queries[block_index * block_rows:(block_index + 1) * block_rows]
        query_heads = query_heads.reshape(block_rows, HEADS, head_dim).astype(jnp.float32)
        scores = jnp.einsum('ihd,jhd->hij', query_heads, key_heads) * head_dim ** (-0.5)
        rows_at = block_index * block_rows + jnp.arange(block_rows, dtype=jnp.int32)
        visible = (columns[None, :] <= rows_at[:, None]) & (columns[None, :] < valid_len)
        weights = jnp.where(visible[None], jax.nn.silu(scores), 0.0).astype(jnp.bfloat16)
        weights = lax.optimization_barrier(weights)
        mixed_heads = jnp.einsum('hij,jhd->ihd', weights.astype(jnp.float32), value_heads)
        outputs.append(mixed_heads.reshape(block_rows, model_width))
    attended = jnp.concatenate(outputs, axis=0)
    inv_rms = lax.rsqrt(lax.optimization_barrier(jnp.mean(attended * attended, axis=1, keepdims=True)) + EPSILON)
    gated_out = (attended * inv_rms * norm_gain.astype(jnp.float32) * gate_part).astype(jnp.bfloat16)
    return tokens.astype(jnp.float32) + jnp.dot(gated_out, w_out, preferred_element_type=jnp.float32)

def pool_sessions(enc_state, valid_len, sess_lens):
    length = enc_state.shape[0]
    sess_ends = jnp.cumsum(sess_lens).astype(jnp.int32)
    sess_starts = sess_ends - sess_lens.astype(jnp.int32)
    positions = jnp.arange(length, dtype=jnp.int32)
    membership = ((positions[None, :] >= sess_starts[:, None]) & (positions[None, :] < sess_ends[:, None]) & (positions[None, :] < valid_len)).astype(jnp.float32)
    sess_sums = jnp.dot(membership, enc_state, precision=lax.Precision.HIGHEST)
    sess_counts = lax.optimization_barrier(jnp.sum(membership, axis=1, keepdims=True))
    return (sess_sums / jnp.maximum(sess_counts, 1.0)).astype(jnp.bfloat16)

def reference(events, hist_len, sess_len, w_uvqk, w_out, attn_gain, w_in, ffn_gain, w_up, w_down):

    def one_user(user_items):
        tokens, valid_len, sess_lens = user_items
        enc_state = encode_user(tokens, valid_len, w_uvqk, w_out, attn_gain)
        return pool_sessions(enc_state, valid_len, sess_lens)
    pooled = lax.map(one_user, (events, hist_len, sess_len))
    micro_count = SESS // MICRO
    micro_rows = pooled[:, :micro_count].reshape(USERS * micro_count, E)
    hidden_in = jnp.dot(micro_rows, w_in, preferred_element_type=jnp.float32)
    inv_rms = lax.rsqrt(lax.optimization_barrier(jnp.mean(hidden_in * hidden_in, axis=1, keepdims=True)) + EPSILON)
    normed = (hidden_in * inv_rms * ffn_gain.astype(jnp.float32)).astype(jnp.bfloat16)
    up_proj = jnp.dot(normed, w_up, preferred_element_type=jnp.float32)
    hidden = jax.nn.gelu(up_proj, approximate=True).astype(jnp.bfloat16)
    cross_out = (hidden_in + jnp.dot(hidden, w_down, preferred_element_type=jnp.float32)).astype(jnp.bfloat16)
    return (pooled.reshape(USERS * SESS, E), cross_out)
```

```python
import jax
import jax.numpy as jnp
from jax import lax
from jax.experimental import pallas as pl
from jax.experimental.pallas import tpu as pltpu
from jax.sharding import PartitionSpec as P

MESH = pl.DeviceIdType.MESH
BF = jnp.bfloat16
F32 = jnp.float32
EPSILON = 1e-06
DMA = pltpu.SemaphoreType.DMA


def dot(a, b):
    return jnp.dot(a, b, preferred_element_type=F32)


def dot_nt(a, b):
    return lax.dot_general(a, b, (((1,), (1,)), ((), ())), preferred_element_type=F32)


def silu(v):
    half = 0.5 * v
    return half + half * jnp.tanh(half)


def kernel(
    events, hist, sess, w_uvqk, w_out, gain, w_in, ffn_gain, w_up, w_down,
    pooled_out, cross_out,
    ev, wa, wo, wi, wu, wd, qs, ks, vs, gs, att, gated, member, rows, hin, part, recv, parts,
    loc, z_s, z_r, zo_s, zo_r, a1_s, a1_r, ao_s, ao_r, a2_s, a2_r, pa_s, pa_r, po_s, po_r,
    b1_s, b1_r, b2_s, b2_r, pb_s, pb_r, pw_s, pw_r, r_s, r_r, c_s, c_r,
):
    s = lax.axis_index("section")
    z = lax.axis_index("dp")
    m = lax.axis_index("mp")
    x = lax.rem(m, 4)
    y = m // 4
    first = (1 - s) * x + s * y
    partner = (1 - s, z, m)

    def spot(d, e):
        xx = lax.rem(x + (1 - s) * d + s * e, 4)
        yy = lax.rem(y + s * d + (1 - s) * e, 4)
        return yy * 4 + xx

    def remote(src, dst, ss, rs, to):
        return pltpu.make_async_remote_copy(
            src_ref=src, dst_ref=dst, send_sem=ss, recv_sem=rs, device_id=to, device_id_type=MESH
        )

    col_a = pl.ds(pl.multiple_of(m * 128, 128), 128)
    col_o = pl.ds(pl.multiple_of(first * 128, 128), 128)
    locals_ = [
        pltpu.make_async_copy(w_uvqk.at[s, :, col_a], wa.at[z, s, :, col_a], loc.at[0]),
        pltpu.make_async_copy(w_out.at[s, :, col_o], wo.at[z, s, :, col_o], loc.at[1]),
        pltpu.make_async_copy(events.at[0], ev, loc.at[2]),
        pltpu.make_async_copy(w_in, wi.at[pl.ds(0, 512), pl.ds((16 * s + m) * 128, 128)], loc.at[3]),
        pltpu.make_async_copy(w_up, wu.at[s], loc.at[4]),
        pltpu.make_async_copy(w_down, wd.at[s], loc.at[5]),
    ]
    for c in locals_:
        c.start()

    barrier = pltpu.get_barrier_semaphore()

    @pl.loop(1, 16)
    def _(d):
        pl.semaphore_signal(barrier, inc=1, device_id=(s, lax.rem(z + d, 16), m), device_id_type=MESH)
        pl.semaphore_signal(barrier, inc=1, device_id=(s, z, lax.rem(m + d, 16)), device_id_type=MESH)

    pl.semaphore_signal(barrier, inc=1, device_id=partner, device_id_type=MESH)

    mine = pl.ds(pl.multiple_of((16 * s + m) * 128, 128), 128)
    wi[pl.ds(512, 16), mine] = jnp.broadcast_to(ffn_gain[...], (16, 128))

    lens = jnp.broadcast_to(sess[...], (32, 32))
    at = lax.broadcasted_iota(jnp.int32, (32, 32), 0)
    of = lax.broadcasted_iota(jnp.int32, (32, 32), 1)
    ends = jnp.sum(jnp.where(of <= at, lens, 0).astype(F32), axis=1, keepdims=True)
    starts = jnp.sum(jnp.where(of < at, lens, 0).astype(F32), axis=1, keepdims=True)
    pos = lax.broadcasted_iota(jnp.int32, (32, 1024), 1).astype(F32)
    limit = jnp.minimum(ends, jnp.broadcast_to(hist[...], (32, 1)).astype(F32))
    inside = (pos >= starts) & (pos < limit)
    member[...] = jnp.where(inside, 1.0, 0.0).astype(BF)
    counts = jnp.maximum(limit - starts, 1.0)

    locals_[0].wait()
    locals_[1].wait()
    pl.semaphore_wait(barrier, 31)


    def z_copy(src_z, d, to_z):
        return remote(
            wa.at[src_z, s, :, col_a], wa.at[src_z, s, :, col_a], z_s.at[d], z_r.at[src_z], (s, to_z, m)
        )

    def zo_copy(src_z, d, to_z):
        return remote(
            wo.at[src_z, s, :, col_o], wo.at[src_z, s, :, col_o], zo_s.at[d], zo_r.at[src_z], (s, to_z, m)
        )

    @pl.loop(1, 16)
    def _(d):
        to = lax.rem(z + d, 16)
        z_copy(z, d, to).start()
        zo_copy(z, d, to).start()

    pw = [
        remote(w_up, wu.at[s], pw_s.at[0], pw_r.at[0], partner),
        remote(w_down, wd.at[s], pw_s.at[1], pw_r.at[1], partner),
    ]
    for c in pw:
        c.start()

    home, inner = z // 4, lax.rem(z, 4)
    step = 1 - 2 * ((5 - inner) // 4)
    groups = [home, lax.rem(home + step + 4, 4), lax.rem(home - step + 4, 4), lax.rem(home + 2, 4)]

    def block(g, mm):
        return wa.at[pl.ds(4 * g, 4), s, :, pl.ds(pl.multiple_of(mm * 128, 128), 128)]

    def oblock(g, ff):
        return wo.at[pl.ds(4 * g, 4), s, :, pl.ds(pl.multiple_of(ff * 128, 128), 128)]

    def a1(i, d):
        b = block(groups[i], m)
        return remote(b, b, a1_s.at[i, d - 1], a1_r.at[i, d - 1], (s, z, spot(d, 0)))

    def ao(i, d):
        b = oblock(groups[i], first)
        return remote(b, b, ao_s.at[i, d - 1], ao_r.at[i, d - 1], (s, z, spot(d, 0)))

    def a1_got(i, d):
        b = block(groups[i], spot(4 - d, 0))
        return remote(b, b, a1_s.at[i, d - 1], a1_r.at[i, d - 1], partner)

    def ao_got(i, d):
        b = oblock(groups[i], lax.rem(first + 4 - d, 4))
        return remote(b, b, ao_s.at[i, d - 1], ao_r.at[i, d - 1], partner)

    def a2(i, d, e):
        b = block(groups[i], spot(4 - d, 0))
        return remote(b, b, a2_s.at[i, d, e - 1], a2_r.at[i, d, e - 1], (s, z, spot(0, e)))

    def a2_got(i, d, e):
        b = block(groups[i], spot(4 - d, 4 - e))
        return remote(b, b, a2_s.at[i, d, e - 1], a2_r.at[i, d, e - 1], partner)

    for i in range(4):
        g = groups[i]
        for k in range(1 if i == 0 else 0, 4):
            src = 4 * g + (lax.rem(inner + k, 4) if i == 0 else k)
            z_copy(src, 0, z).wait_recv()
            zo_copy(src, 0, z).wait_recv()
        for d in range(1, 4):
            a1(i, d).start()
            ao(i, d).start()
        for e in range(1, 4):
            a2(i, 0, e).start()

    def pa(i, side):
        b = wa.at[pl.ds(4 * groups[i], 4), side]
        return remote(b, b, pa_s.at[i], pa_r.at[i], partner)

    def po(i, side):
        b = wo.at[pl.ds(4 * groups[i], 4), side]
        return remote(b, b, po_s.at[i], po_r.at[i], partner)

    for i in range(4):
        for d in range(1, 4):
            a1_got(i, d).wait_recv()
            for e in range(1, 4):
                a2(i, d, e).start()
        for d in range(1, 4):
            ao_got(i, d).wait_recv()
        po(i, s).start()

    locals_[3].wait()

    def win(mm, side):
        return wi.at[:, pl.ds(pl.multiple_of((16 * side + mm) * 128, 128), 128)]

    def b1(d):
        b = win(m, s)
        return remote(b, b, b1_s.at[d - 1], b1_r.at[d - 1], (s, z, spot(d, 0)))

    def b1_got(d):
        b = win(spot(4 - d, 0), s)
        return remote(b, b, b1_s.at[d - 1], b1_r.at[d - 1], partner)

    def b2(d, e):
        b = win(spot(4 - d, 0), s)
        return remote(b, b, b2_s.at[d, e - 1], b2_r.at[d, e - 1], (s, z, spot(0, e)))

    def b2_got(d, e):
        b = win(spot(4 - d, 4 - e), s)
        return remote(b, b, b2_s.at[d, e - 1], b2_r.at[d, e - 1], partner)

    def pb(side):
        b = wi.at[:, pl.ds(pl.multiple_of(side * 2048, 128), 2048)]
        return remote(b, b, pb_s, pb_r, partner)

    for d in range(1, 4):
        b1(d).start()
    for e in range(1, 4):
        b2(0, e).start()

    for i in range(4):
        for d in range(4):
            for e in range(1, 4):
                a2_got(i, d, e).wait_recv()
        pa(i, s).start()

    for d in range(1, 4):
        b1_got(d).wait_recv()
        for e in range(1, 4):
            b2(d, e).start()

    locals_[2].wait()
    for i in range(4):
        pa(i, 1 - s).wait_recv()
        po(i, 1 - s).wait_recv()

    valid = jnp.broadcast_to(hist[...], (256, 1))

    def project(r):
        at_rows = pl.ds(pl.multiple_of(r * 256, 256), 256)
        tokens = ev[at_rows, :]
        row = r * 256 + lax.broadcasted_iota(jnp.int32, (256, 1), 0)

        def part_of(c):
            w = wa[:, :, :, pl.ds(512 * c, 512)].reshape(512, 512)
            return silu(dot(tokens, w))

        gs[at_rows, :] = part_of(0)
        vs[at_rows, :] = jnp.where(row < valid, part_of(1), 0.0).astype(BF)
        qs[at_rows, :] = (part_of(2) * (0.5 * 128 ** (-0.5))).astype(BF)
        ks[at_rows, :] = part_of(3).astype(BF)

    def attend(i):
        lo = i * 256
        diagonal = lax.broadcasted_iota(jnp.int32, (256, 256), 1) <= lax.broadcasted_iota(
            jnp.int32, (256, 256), 0
        )

        @pl.loop(0, 4)
        def _(h):
            cols = pl.ds(pl.multiple_of(h * 128, 128), 128)
            q = qs[pl.ds(lo, 256), cols]

            def weigh(j):
                u = dot_nt(q, ks[pl.ds(256 * j, 256), cols])
                return u + u * jnp.tanh(u)

            acc = dot(
                jnp.where(diagonal, weigh(i), 0.0).astype(BF), vs[pl.ds(lo, 256), cols]
            )
            for j in range(i):
                acc += dot(weigh(j).astype(BF), vs[pl.ds(256 * j, 256), cols])
            att[pl.ds(lo, 256), cols] = acc

    def gate(i):
        at_rows = pl.ds(i * 256, 256)
        a = att[at_rows, :]
        inv = lax.rsqrt(jnp.mean(a * a, axis=1, keepdims=True) + EPSILON)
        gated[at_rows, :] = (a * inv * gain[...] * gs[at_rows, :]).astype(BF)

    def pool(r0, nr, upto):
        mm = member[pl.ds(r0, nr), pl.ds(0, upto)]
        pe = dot(mm, ev[pl.ds(0, upto), :])
        pg = dot(mm, gated[pl.ds(0, upto), :])
        hi = pg.astype(BF)
        lo = (pg - hi.astype(F32)).astype(BF)
        w = wo[...].reshape(512, 512)
        return pe + dot(hi, w) + dot(lo, w)

    for r in range(2):
        project(r)
    for i in range(2):
        attend(i)
        gate(i)
    early = (pool(0, 16, 512) / counts[0:16])[0:8].astype(BF)
    rows[m] = early

    def r_copy(d, slot, to):
        return remote(rows.at[slot], rows.at[slot], r_s.at[d], r_r.at[d], (s, z, to))

    @pl.loop(1, 16)
    def _(d):
        r_copy(d, m, lax.rem(m + d, 16)).start()

    for r in range(2, 4):
        project(r)
    for i in range(2, 4):
        attend(i)
        gate(i)
    parts[...] = pool(0, 32, 1024) / counts
    pooled_out[...] = parts[...].astype(BF)

    for d in range(4):
        for e in range(1, 4):
            b2_got(d, e).wait_recv()
    pb(s).start()

    @pl.loop(1, 16)
    def _(d):
        r_copy(d, lax.rem(m + 16 - d, 16), m).wait_recv()

    locals_[4].wait()
    locals_[5].wait()
    for k, c in enumerate(pw):
        c.wait_recv()
    pb(1 - s).wait_recv()

    xs = rows[...].astype(F32).reshape(128, 512).astype(BF)

    def widen(c, carry):
        acc, sq = carry
        cols = pl.ds(pl.multiple_of(c * 512, 512), 512)
        h = dot(xs, wi[pl.ds(0, 512), cols])
        hin[:, cols] = h
        g = wi[pl.ds(512, 16), cols].astype(F32)[0:1]
        at_k = pl.ds(pl.multiple_of(lax.rem(c, 4) * 512, 512), 512)
        acc += dot((h * g).astype(BF), wu[c // 4, at_k, :])
        return acc, sq + jnp.sum(h * h, axis=1, keepdims=True)

    acc, sq = lax.fori_loop(
        0, 8, widen, (jnp.zeros((128, 512), F32), jnp.zeros((128, 1), F32))
    )
    up = acc * lax.rsqrt(sq * (1.0 / 4096) + EPSILON)
    hidden = jax.nn.gelu(up, approximate=True).astype(BF)

    def c_copy(half, d, src, dst, to):
        cols = pl.ds(half * 2048, 2048)
        return remote(
            part.at[src, :, cols], recv.at[dst, :, cols], c_s.at[half, d], c_r.at[half, d], (s, z, to)
        )

    for half in range(2):

        @pl.loop(0, 4)
        def _(c):
            cols = pl.ds(pl.multiple_of(half * 2048 + c * 512, 512), 512)
            p = dot(hidden, wd[half, :, pl.ds(pl.multiple_of(c * 512, 512), 512)])
            part[:, :, cols] = p.reshape(16, 8, 512).astype(BF)

        @pl.loop(1, 16)
        def _(d):
            to = lax.rem(m + d, 16)
            c_copy(half, d, to, m, to).start()

    for half in range(2):
        cols = pl.ds(half * 2048, 2048)
        total = hin[pl.ds(pl.multiple_of(m * 8, 8), 8), cols] + part[m, :, cols].astype(F32)

        def gather(d, total):
            src = lax.rem(m + 16 - d, 16)
            c_copy(half, d, 0, src, m).wait_recv()
            return total + recv[src, :, cols].astype(F32)

        total = lax.fori_loop(1, 16, gather, total)
        cross_out[:, cols] = total.astype(BF)

    @pl.loop(1, 16)
    def _(d):
        z_copy(z, d, z).wait_send()
        zo_copy(z, d, z).wait_send()
        r_copy(d, m, m).wait_send()
        c_copy(0, d, 0, m, m).wait_send()
        c_copy(1, d, 0, m, m).wait_send()

    for c in pw:
        c.wait_send()
    for i in range(4):
        for d in range(1, 4):
            a1(i, d).wait_send()
            ao(i, d).wait_send()
        for d in range(4):
            for e in range(1, 4):
                a2(i, d, e).wait_send()
        pa(i, s).wait_send()
        po(i, s).wait_send()
    for d in range(1, 4):
        b1(d).wait_send()
    for d in range(4):
        for e in range(1, 4):
            b2(d, e).wait_send()
    pb(s).wait_send()


def per_device(events, hist_len, sess_len, w_uvqk, w_out, attn_gain, w_in, ffn_gain, w_up, w_down):
    anywhere = pl.BlockSpec(memory_space=pl.ANY)
    inside = pl.BlockSpec(memory_space=pltpu.VMEM)
    vm = pltpu.VMEM
    return pl.pallas_call(
        kernel,
        out_shape=(jax.ShapeDtypeStruct((32, 512), BF), jax.ShapeDtypeStruct((8, 4096), BF)),
        in_specs=[
            anywhere, inside, inside, anywhere, anywhere, inside, anywhere, inside, anywhere, anywhere,
        ],
        out_specs=(inside, inside),
        scratch_shapes=[
            vm((1024, 512), BF),
            vm((16, 2, 16, 2048), BF),
            vm((16, 2, 16, 512), BF),
            vm((528, 4096), BF),
            vm((2, 2048, 512), BF),
            vm((2, 512, 2048), BF),
            vm((1024, 512), BF),
            vm((1024, 512), BF),
            vm((1024, 512), BF),
            vm((1024, 512), F32),
            vm((1024, 512), F32),
            vm((1024, 512), BF),
            vm((32, 1024), BF),
            vm((16, 8, 512), BF),
            vm((128, 4096), F32),
            vm((16, 8, 4096), BF),
            vm((16, 8, 4096), BF),
            vm((32, 512), F32),
            DMA((6,)),
            DMA((16,)), DMA((16,)), DMA((16,)), DMA((16,)),
            DMA((4, 3)), DMA((4, 3)), DMA((4, 3)), DMA((4, 3)),
            DMA((4, 4, 3)), DMA((4, 4, 3)),
            DMA((4,)), DMA((4,)), DMA((4,)), DMA((4,)),
            DMA((3,)), DMA((3,)), DMA((4, 3)), DMA((4, 3)),
            DMA, DMA,
            DMA((2,)), DMA((2,)),
            DMA((16,)), DMA((16,)),
            DMA((2, 16)), DMA((2, 16)),
        ],
        compiler_params=pltpu.CompilerParams(
            collective_id=0, has_side_effects=True, vmem_limit_bytes=60 << 20
        ),
        name="encode_and_mix",
    )(
        events, hist_len.reshape(1, 1), sess_len, w_uvqk.reshape(2, 16, 2048), w_out.reshape(2, 16, 512),
        attn_gain.reshape(1, 512), w_in, ffn_gain, w_up, w_down,
    )


def solution(mesh):
    return jax.shard_map(
        per_device,
        mesh=mesh,
        in_specs=(
            P(("section", "dp", "mp"), None, None),
            P(("section", "dp", "mp")),
            P(("section", "dp", "mp"), None),
            P("dp", None),
            P("dp", None),
            P(),
            P(None, ("section", "mp")),
            P(None, ("section", "mp")),
            P("section", "mp"),
            P("mp", "section"),
        ),
        out_specs=(P(("section", "dp", "mp"), None), P(("section", "dp", "mp"), None)),
        check_vma=False,
    )
```

```python
import jax
import jax.numpy as jnp
from jax import lax
from jax.experimental import pallas as pl
from jax.experimental.pallas import tpu as pltpu
from jax.sharding import PartitionSpec as P

MESH = pl.DeviceIdType.MESH
BF = jnp.bfloat16
F32 = jnp.float32
EPSILON = 1e-06
DMA = pltpu.SemaphoreType.DMA


def dot(a, b):
    return jnp.dot(a, b, preferred_element_type=F32)


def dot_nt(a, b):
    return lax.dot_general(a, b, (((1,), (1,)), ((), ())), preferred_element_type=F32)


def silu(v):
    half = 0.5 * v
    return half + half * jnp.tanh(half)


def kernel(
    events, hist, sess, w_uvqk, w_out, gain, w_in, ffn_gain, w_up, w_down,
    pooled_out, cross_out,
    hist_v, sess_v, gain_v, fgain_v, pooled_v, cross_v,
    ev, wa, wo, wi, wu, wd, qs, ks, vs, gs, att, gated, member, rows, hin, part, recv, relay, last, own,
    pre, loc, z_s, z_r, zo_s, zo_r, a1_s, a1_r, ao_s, ao_r, a2_s, a2_r, pa_s, pa_r, po_s, po_r,
    b_s, f_s, b1_r, f1_r, b2_r, f2_r, pb_s, pb_r, pu_s, pu_r, pd_s, pd_r, r_s, r_r,
    c1_s, c1_r, c2_s, c2_r, out_s,
):
    s = lax.axis_index("section")
    z = lax.axis_index("dp")
    m = lax.axis_index("mp")
    x = lax.rem(m, 4)
    y = m // 4
    first = (1 - s) * x + s * y
    second = s * x + (1 - s) * y
    partner = (1 - s, z, m)

    barrier = pltpu.get_barrier_semaphore()

    @pl.loop(1, 16)
    def _(d):
        pl.semaphore_signal(barrier, inc=1, device_id=(s, lax.rem(z + d, 16), m), device_id_type=MESH)
        pl.semaphore_signal(barrier, inc=1, device_id=(s, z, lax.rem(m + d, 16)), device_id_type=MESH)

    pl.semaphore_signal(barrier, inc=1, device_id=partner, device_id_type=MESH)

    def spot(d, e):
        xx = lax.rem(x + (1 - s) * d + s * e, 4)
        yy = lax.rem(y + s * d + (1 - s) * e, 4)
        return yy * 4 + xx

    def remote(src, dst, ss, rs, to):
        return pltpu.make_async_remote_copy(
            src_ref=src, dst_ref=dst, send_sem=ss, recv_sem=rs, device_id=to, device_id_type=MESH
        )

    def lane(k):
        return pl.ds(pl.multiple_of(k * 128, 128), 128)

    small = [
        pltpu.make_async_copy(ffn_gain, fgain_v, loc.at[6]),
        pltpu.make_async_copy(sess, sess_v, loc.at[7]),
        pltpu.make_async_copy(hist, hist_v, loc.at[8]),
        pltpu.make_async_copy(gain, gain_v, loc.at[9]),
    ]
    locals_ = [
        pltpu.make_async_copy(w_uvqk.at[s, :, lane(m)], wa.at[z, s, :, lane(m)], loc.at[0]),
        pltpu.make_async_copy(w_out.at[s, :, lane(first)], wo.at[z, s, :, lane(first)], loc.at[1]),
        pltpu.make_async_copy(w_in, wi.at[pl.ds(0, 512), lane(16 * s + m)], loc.at[3]),
        pltpu.make_async_copy(events.at[0], ev, loc.at[2]),
        pltpu.make_async_copy(w_up, wu.at[s], loc.at[4]),
        pltpu.make_async_copy(w_down, wd.at[s], loc.at[5]),
    ]
    for c in locals_[:2] + small + locals_[2:]:
        c.start()

    pl.semaphore_wait(barrier, 31)
    locals_[0].wait()

    def z_copy(to_z):
        b = wa.at[z, s, :, lane(m)]
        return remote(b, b, z_s, z_r.at[z // 4], (s, to_z, m))

    def zo_copy(to_z):
        b = wo.at[z, s, :, lane(first)]
        return remote(b, b, zo_s, zo_r, (s, to_z, m))

    def arrived(ref, sem):
        remote(ref, ref, sem, sem, partner).wait_recv()

    def sent(ref, sem):
        remote(ref, ref, sem, sem, partner).wait_send()

    @pl.loop(1, 16)
    def _(d):
        z_copy(lax.rem(z + d, 16)).start()

    small[0].wait()
    wi[pl.ds(512, 16), lane(16 * s + m)] = jnp.broadcast_to(fgain_v[...], (16, 128))
    locals_[1].wait()
    locals_[2].wait()

    def win(mm, side):
        return wi.at[:, lane(16 * side + mm)]

    def half_win(mm, up):
        return wi.at[pl.ds(0, 256) if up > 0 else pl.ds(256, 272), lane(16 * s + mm)]

    def b1(up):
        b = win(m, s)
        return remote(b, b, b_s, b1_r.at[up], (s, z, spot(1 if up else 3, 0)))

    def b1_got(up):
        arrived(win(spot(3 if up else 1, 0), s), b1_r.at[up])

    def f1(up):
        b = half_win(spot(3 if up else 1, 0), up)
        return remote(b, b, f_s, f1_r, (s, z, spot(1 if up else 3, 0)))

    def f1_got():
        arrived(win(spot(2, 0), s), f1_r)

    def b2(d, up):
        b = win(spot(d, 0), s)
        return remote(b, b, b_s, b2_r.at[d, up], (s, z, spot(0, 1 if up else 3)))

    def b2_got(d, up):
        arrived(win(spot(d, 3 if up else 1), s), b2_r.at[d, up])

    def f2(d, up):
        b = half_win(spot(d, 3 if up else 1), up)
        return remote(b, b, f_s, f2_r.at[d], (s, z, spot(0, 1 if up else 3)))

    def f2_got(d):
        arrived(win(spot(d, 2), s), f2_r.at[d])

    def pb(d, e):
        b = win(spot(d, e), s)
        return remote(b, b, pb_s, pb_r, partner)

    for up in range(2):
        b1(up).start()
    for up in range(2):
        b2(0, up).start()

    pw = [
        remote(w_up, wu.at[s], pu_s, pu_r, partner),
        remote(w_down, wd.at[s], pd_s, pd_r, partner),
    ]
    pb(0, 0).start()
    for c in pw:
        c.start()

    @pl.loop(1, 16)
    def _(d):
        zo_copy(lax.rem(z + d, 16)).start()

    small[1].wait()
    small[2].wait()
    lens = jnp.broadcast_to(sess_v[...], (32, 32))
    at = lax.broadcasted_iota(jnp.int32, (32, 32), 0)
    of = lax.broadcasted_iota(jnp.int32, (32, 32), 1)
    ends = jnp.sum(jnp.where(of <= at, lens, 0).astype(F32), axis=1, keepdims=True)
    starts = jnp.sum(jnp.where(of < at, lens, 0).astype(F32), axis=1, keepdims=True)
    pos = lax.broadcasted_iota(jnp.int32, (32, 1024), 1).astype(F32)
    limit = jnp.minimum(ends, jnp.broadcast_to(hist_v[...], (32, 1)).astype(F32))
    inside = (pos >= starts) & (pos < limit)
    member[...] = jnp.where(inside, 1.0, 0.0).astype(BF)
    counts = jnp.maximum(limit - starts, 1.0)

    home, inner = z // 4, lax.rem(z, 4)
    step = 1 - 2 * ((5 - inner) // 4)
    groups = [home, lax.rem(home + step + 4, 4), lax.rem(home - step + 4, 4), lax.rem(home + 2, 4)]

    def block(g, mm):
        return wa.at[pl.ds(4 * g, 4), s, :, lane(mm)]

    def a1(i, d):
        b = block(groups[i], m)
        return remote(b, b, a1_s, a1_r.at[i], (s, z, spot(d, 0)))

    def a2(i, d, e):
        b = block(groups[i], spot(4 - d, 0))
        return remote(b, b, a2_s, a2_r.at[i], (s, z, spot(0, e)))

    def pa(i, side):
        b = wa.at[pl.ds(4 * groups[i], 4), side]
        return remote(b, b, pa_s, pa_r.at[i], partner)

    def oblock(ff):
        return wo.at[:, s, :, lane(ff)]

    def ao(d):
        b = oblock(first)
        return remote(b, b, ao_s, ao_r, (s, z, spot(d, 0)))

    def po(side):
        b = wo.at[:, side]
        return remote(b, b, po_s, po_r, partner)

    def from_z(i):
        g = groups[i]
        arrived(wa.at[pl.ds(4 * g, 3 if i == 0 else 4), s, :, lane(m)], z_r.at[g])
        for d in range(1, 4):
            a1(i, d).start()
        for e in range(1, 4):
            a2(i, 0, e).start()

    def from_first(i):
        arrived(wa.at[pl.ds(4 * groups[i], 4), s, :, pl.ds(0, 3 * 128)], a1_r.at[i])
        for d in range(1, 4):
            for e in range(1, 4):
                a2(i, d, e).start()

    def from_second(i):
        arrived(wa.at[pl.ds(4 * groups[i], 4), s, :, pl.ds(0, 12 * 128)], a2_r.at[i])
        pa(i, s).start()

    def pass_on(d):
        for up in range(2):
            b2_got(d, up)
            f2(d, up).start()
            pb(d, 3 if up else 1).start()

    def complete(d):
        f2_got(d)
        pb(d, 2).start()

    from_z(0)
    for up in range(2):
        b1_got(up)
        f1(up).start()
    from_z(1)
    from_first(0)
    from_z(2)
    from_first(1)
    from_z(3)
    from_first(2)
    from_first(3)
    for d in (3, 1):
        for up in range(2):
            b2(d, up).start()
        pb(d, 0).start()
    f1_got()
    for up in range(2):
        b2(2, up).start()
    pb(2, 0).start()
    arrived(wo.at[pl.ds(0, 15), s, :, lane(first)], zo_r)
    for d in range(1, 4):
        ao(d).start()
    from_second(0)
    from_second(1)
    from_second(2)
    locals_[3].wait()
    for i in range(2):
        pa(i, 1 - s).wait_recv()

    def tokens_of(lo, i, j):
        at_rows = pl.ds(lo, 256)
        return jnp.concatenate([ev[at_rows, lane(groups[i])], ev[at_rows, lane(groups[j])]], axis=1)

    def weights_of(c, i, j):
        cols = pl.ds(512 * c, 512)
        return jnp.concatenate(
            [wa[pl.ds(4 * groups[k], 4), :, :, cols].reshape(128, 512) for k in (i, j)], axis=0
        )

    for c in range(4):
        w = weights_of(c, 0, 1)
        for r in range(2):
            pre[pl.ds(256 * r, 256), pl.ds(512 * c, 512)] = dot(tokens_of(256 * r, 0, 1), w)

    from_second(3)
    pass_on(0)

    for i in range(2, 4):
        pa(i, 1 - s).wait_recv()

    small[3].wait()
    valid = jnp.broadcast_to(hist_v[...], (256, 1))

    def keep(r, parts):
        at_rows = pl.ds(r * 256, 256)
        row = r * 256 + lax.broadcasted_iota(jnp.int32, (256, 1), 0)
        gs[at_rows, :] = parts(0)
        vs[at_rows, :] = jnp.where(row < valid, parts(1), 0.0).astype(BF)
        qs[at_rows, :] = (parts(2) * (0.5 * 128 ** (-0.5))).astype(BF)
        ks[at_rows, :] = parts(3).astype(BF)

    def project(r):
        tokens = ev[pl.ds(r * 256, 256), :]
        keep(r, lambda c: silu(dot(tokens, wa[:, :, :, pl.ds(512 * c, 512)].reshape(512, 512))))

    def project_rest(r):
        tokens = tokens_of(256 * r, 2, 3)
        keep(
            r,
            lambda c: silu(
                pre[pl.ds(256 * r, 256), pl.ds(512 * c, 512)] + dot(tokens, weights_of(c, 2, 3))
            ),
        )

    diagonal = lax.broadcasted_iota(jnp.int32, (256, 256), 1) <= lax.broadcasted_iota(
        jnp.int32, (256, 256), 0
    )

    def attend(i, heads):
        lo = i * 256
        for h in heads:
            cols = pl.ds(h * 128, 128)
            q = qs[pl.ds(lo, 256), cols]

            def weigh(j):
                u = dot_nt(q, ks[pl.ds(256 * j, 256), cols])
                return u + u * jnp.tanh(u)

            acc = dot(
                jnp.where(diagonal, weigh(i), 0.0).astype(BF), vs[pl.ds(lo, 256), cols]
            )
            for j in range(i):
                acc += dot(weigh(j).astype(BF), vs[pl.ds(256 * j, 256), cols])
            att[pl.ds(lo, 256), cols] = acc

    def gate(i):
        at_rows = pl.ds(i * 256, 256)
        a = att[at_rows, :]
        inv = lax.rsqrt(jnp.mean(a * a, axis=1, keepdims=True) + EPSILON)
        gated[at_rows, :] = (a * inv * gain_v[...] * gs[at_rows, :]).astype(BF)

    def pool(nr, upto):
        mm = member[pl.ds(0, nr), pl.ds(0, upto)]
        pe = dot(mm, ev[pl.ds(0, upto), :])
        pg = dot(mm, gated[pl.ds(0, upto), :])
        hi = pg.astype(BF)
        lo = (pg - hi.astype(F32)).astype(BF)
        w = wo[...].reshape(512, 512)
        return pe + dot(hi, w) + dot(lo, w)

    for r in range(2):
        project_rest(r)
    arrived(wo.at[:, s, :, pl.ds(0, 3 * 128)], ao_r)
    po(s).start()
    pass_on(3)
    pass_on(1)
    for i in range(2):
        attend(i, range(4))
        gate(i)
    pass_on(2)
    complete(0)
    po(1 - s).wait_recv()
    early = (pool(16, 512) / counts[0:16])[0:8].astype(BF)
    slot = 4 * first + second
    rows[slot] = early

    def r_copy(to):
        return remote(rows.at[slot], rows.at[slot], r_s, r_r, (s, z, to))

    @pl.loop(1, 16)
    def _(d):
        r_copy(lax.rem(m + d, 16)).start()

    complete(3)
    complete(1)
    project(2)
    complete(2)
    project(3)

    arrived(rows.at[pl.ds(0, 15)], r_r)
    locals_[4].wait()
    locals_[5].wait()
    for c in pw:
        c.wait_recv()
    arrived(wi.at[:, pl.ds(pl.multiple_of((1 - s) * 2048, 128), 2048)], pb_r)

    xs = rows[...].astype(F32).reshape(128, 512).astype(BF)
    acc = jnp.zeros((128, 512), F32)
    sq = jnp.zeros((128, 1), F32)
    for c in range(8):
        cols = pl.ds(c * 512, 512)
        h = dot(xs, wi[pl.ds(0, 512), cols])
        hin[:, cols] = h
        g = wi[pl.ds(512, 16), cols].astype(F32)[0:1]
        acc += dot((h * g).astype(BF), wu[c // 4, pl.ds((c % 4) * 512, 512), :])
        sq += jnp.sum(h * h, axis=1, keepdims=True)
    up = acc * lax.rsqrt(sq * (1.0 / 4096) + EPSILON)
    hidden = jax.nn.gelu(up, approximate=True).astype(BF)

    def chunk(k):
        return pl.ds(k * 1024, 1024)

    def c1(k, d):
        to_first = lax.rem(first + d, 4)
        return remote(
            part.at[pl.ds(4 * to_first, 4), :, chunk(k)], recv.at[d - 1, :, :, chunk(k)],
            c1_s, c1_r.at[k], (s, z, spot(d, 0)),
        )

    def c2(k, e):
        return remote(
            relay.at[e - 1, :, chunk(k)], last.at[e - 1, :, chunk(k)],
            c2_s, c2_r.at[k], (s, z, spot(0, e)),
        )

    for k in range(4):
        p = dot(hidden, wd[k // 2, :, pl.ds((k % 2) * 1024, 1024)])
        part[:, :, chunk(k)] = p.reshape(16, 8, 1024).astype(BF)
        for d in range(1, 4):
            c1(k, d).start()

    def relay_chunk(k):
        arrived(recv.at[:, :, :, chunk(k)], c1_r.at[k])
        for e in (1, 2, 3, 0):
            gg = lax.rem(second + e, 4)
            t = part[4 * first + gg, :, chunk(k)].astype(F32)
            for d in range(1, 4):
                t += recv[d - 1, gg, :, chunk(k)].astype(F32)
            if e:
                relay[e - 1, :, chunk(k)] = t.astype(BF)
                c2(k, e).start()
            else:
                own[:, chunk(k)] = t + hin[pl.ds(pl.multiple_of(slot * 8, 8), 8), chunk(k)]

    def settle():
        sent(wa.at[pl.ds(0, 15), s, :, lane(m)], z_s)
        sent(wo.at[pl.ds(0, 15), s, :, lane(first)], zo_s)
        sent(rows.at[pl.ds(0, 15)], r_s)
        for c in pw:
            c.wait_send()
        sent(wa.at[pl.ds(0, 12), s, :, pl.ds(0, 512)], a1_s)
        sent(wa.at[:, s, :, pl.ds(0, 12 * 128)], a2_s)
        sent(wa.at[:, s], pa_s)
        sent(wo.at[:, s, :, pl.ds(0, 3 * 128)], ao_s)
        po(s).wait_send()
        sent(wi.at[:, pl.ds(0, 10 * 128)], b_s)
        sent(wi.at[:, pl.ds(0, 5 * 128)], f_s)
        sent(wi.at[:, pl.ds(0, 16 * 128)], pb_s)

    attend(2, (0, 1))
    attend(2, (2, 3))
    gate(2)
    relay_chunk(0)
    attend(3, (0, 1))
    relay_chunk(1)
    attend(3, (2, 3))
    relay_chunk(2)
    gate(3)
    pooled_v[...] = (pool(32, 1024) / counts).astype(BF)
    outs = [pltpu.make_async_copy(pooled_v, pooled_out, out_s.at[0])]
    outs[0].start()
    relay_chunk(3)
    settle()
    for k in range(4):
        t = own[:, chunk(k)]
        arrived(last.at[:, :, chunk(k)], c2_r.at[k])
        for e in range(1, 4):
            t += last[e - 1, :, chunk(k)].astype(F32)
        cross_v[:, chunk(k)] = t.astype(BF)
        outs.append(
            pltpu.make_async_copy(cross_v.at[:, chunk(k)], cross_out.at[:, chunk(k)], out_s.at[k + 1])
        )
        outs[-1].start()
    sent(recv, c1_s)
    sent(relay, c2_s)
    for c in outs:
        c.wait()


def hand_on(pooled, cross, pooled_out, cross_out):
    pooled_out[...] = pooled[...]
    cross_out[...] = cross[...]


def per_device(events, hist_len, sess_len, w_uvqk, w_out, attn_gain, w_in, ffn_gain, w_up, w_down):
    anywhere = pl.BlockSpec(memory_space=pl.ANY)
    vm = pltpu.VMEM
    outs = (jax.ShapeDtypeStruct((32, 512), BF), jax.ShapeDtypeStruct((8, 4096), BF))
    both = pl.pallas_call(
        kernel,
        out_shape=outs,
        in_specs=[anywhere] * 10,
        out_specs=(anywhere, anywhere),
        scratch_shapes=[
            vm((1, 1), jnp.int32),
            vm((1, 32), jnp.int32),
            vm((1, 512), F32),
            vm((1, 128), BF),
            vm((32, 512), BF),
            vm((8, 4096), BF),
            vm((1024, 512), BF),
            vm((16, 2, 16, 2048), BF),
            vm((16, 2, 16, 512), BF),
            vm((528, 4096), BF),
            vm((2, 2048, 512), BF),
            vm((2, 512, 2048), BF),
            vm((1024, 512), BF),
            vm((1024, 512), BF),
            vm((1024, 512), BF),
            vm((1024, 512), F32),
            vm((1024, 512), F32),
            vm((1024, 512), BF),
            vm((32, 1024), BF),
            vm((16, 8, 512), BF),
            vm((128, 4096), F32),
            vm((16, 8, 4096), BF),
            vm((3, 4, 8, 4096), BF),
            vm((3, 8, 4096), BF),
            vm((3, 8, 4096), BF),
            vm((8, 4096), F32),
            vm((512, 2048), F32),
            DMA((10,)),
            DMA, DMA((4,)), DMA, DMA,
            DMA, DMA((4,)), DMA, DMA,
            DMA, DMA((4,)),
            DMA, DMA((4,)), DMA, DMA,
            DMA, DMA, DMA((2,)), DMA, DMA((4, 2)), DMA((4,)),
            DMA, DMA,
            DMA, DMA, DMA, DMA,
            DMA, DMA,
            DMA, DMA((4,)), DMA, DMA((4,)),
            DMA((5,)),
        ],
        compiler_params=pltpu.CompilerParams(
            collective_id=0, has_side_effects=True, vmem_limit_bytes=60 << 20
        ),
        name="encode_and_mix",
    )(
        events, hist_len.reshape(1, 1), sess_len, w_uvqk.reshape(2, 16, 2048), w_out.reshape(2, 16, 512),
        attn_gain.reshape(1, 512), w_in, ffn_gain, w_up, w_down,
    )
    return pl.pallas_call(hand_on, out_shape=outs, name="hand_on")(*both)


def solution(mesh):
    return jax.shard_map(
        per_device,
        mesh=mesh,
        in_specs=(
            P(("section", "dp", "mp"), None, None),
            P(("section", "dp", "mp")),
            P(("section", "dp", "mp"), None),
            P("dp", None),
            P("dp", None),
            P(),
            P(None, ("section", "mp")),
            P(None, ("section", "mp")),
            P("section", "mp"),
            P("mp", "section"),
        ),
        out_specs=(P(("section", "dp", "mp"), None), P(("section", "dp", "mp"), None)),
        check_vma=False,
    )
```

```python
import jax
import jax.numpy as jnp
from jax import lax
from jax.experimental import pallas as pl
from jax.experimental.pallas import tpu as pltpu
from jax.sharding import PartitionSpec as P

MESH = pl.DeviceIdType.MESH
BF = jnp.bfloat16
F32 = jnp.float32
EPSILON = 1e-06
DMA = pltpu.SemaphoreType.DMA


def dot(a, b):
    return jnp.dot(a, b, preferred_element_type=F32)


def dot_nt(a, b):
    return lax.dot_general(a, b, (((1,), (1,)), ((), ())), preferred_element_type=F32)


def silu(v, scale=None):
    half = (0.5 * v).astype(BF)
    first = half if scale is None else ((0.5 * scale) * v).astype(BF)
    return first + first * jnp.tanh(half)


def kernel(
    events, hist, sess, w_uvqk, w_out, gain, w_in, ffn_gain, w_up, w_down,
    pooled_out, cross_out,
    hist_s, sess_v, gain_v, fgain_v, pooled_v, cross_v,
    ev, wa, wo, wi, wu, wd, qs, ks, vs, gs, att, gated, member, rows, hin, part, recv, relay, last, own,
    pre, pooled_ev, loc, z_s, z_r, zo_s, zo_r, a1_s, a1_r, ao_s, ao_r, a2_s, a2_r, pa_s, pa_r, po_s, po_r,
    b_s, f_s, b1_r, f1_r, b2_r, f2_r, pb_s, pb_r, pu_s, pu_r, pd_s, pd_r, r_s, r_r,
    c1_s, c1_r, c2_s, c2_r, out_s,
):
    s = lax.axis_index("section")
    z = lax.axis_index("dp")
    m = lax.axis_index("mp")
    x = lax.rem(m, 4)
    y = m // 4
    first = (1 - s) * x + s * y
    second = s * x + (1 - s) * y
    partner = (1 - s, z, m)

    barrier = pltpu.get_barrier_semaphore()

    @pl.loop(1, 16)
    def _(d):
        pl.semaphore_signal(barrier, inc=1, device_id=(s, lax.rem(z + d, 16), m), device_id_type=MESH)
        pl.semaphore_signal(barrier, inc=1, device_id=(s, z, lax.rem(m + d, 16)), device_id_type=MESH)

    pl.semaphore_signal(barrier, inc=1, device_id=partner, device_id_type=MESH)

    def spot(d, e):
        xx = lax.rem(x + (1 - s) * d + s * e, 4)
        yy = lax.rem(y + s * d + (1 - s) * e, 4)
        return yy * 4 + xx

    def remote(src, dst, ss, rs, to):
        return pltpu.make_async_remote_copy(
            src_ref=src, dst_ref=dst, send_sem=ss, recv_sem=rs, device_id=to, device_id_type=MESH
        )

    def lane(k):
        return pl.ds(pl.multiple_of(k * 128, 128), 128)

    small = [
        pltpu.make_async_copy(ffn_gain, fgain_v, loc.at[6]),
        pltpu.make_async_copy(sess, sess_v, loc.at[7]),
        pltpu.make_async_copy(hist, hist_s, loc.at[8]),
        pltpu.make_async_copy(gain, gain_v, loc.at[9]),
    ]
    locals_ = [
        pltpu.make_async_copy(w_uvqk.at[s, :, lane(m)], wa.at[z, s, :, lane(m)], loc.at[0]),
        pltpu.make_async_copy(w_out.at[s, :, lane(first)], wo.at[z, s, :, lane(first)], loc.at[1]),
        pltpu.make_async_copy(w_in, wi.at[pl.ds(0, 512), lane(16 * s + m)], loc.at[3]),
        pltpu.make_async_copy(events.at[0], ev, loc.at[2]),
        pltpu.make_async_copy(w_up, wu.at[s], loc.at[4]),
        pltpu.make_async_copy(w_down, wd.at[s], loc.at[5]),
    ]
    for c in locals_[:2] + small + locals_[2:]:
        c.start()

    pl.semaphore_wait(barrier, 31)
    locals_[0].wait()

    def z_copy(to_z):
        b = wa.at[z, s, :, lane(m)]
        return remote(b, b, z_s, z_r.at[z // 4], (s, to_z, m))

    def zo_copy(to_z):
        b = wo.at[z, s, :, lane(first)]
        return remote(b, b, zo_s, zo_r, (s, to_z, m))

    def arrived(ref, sem):
        remote(ref, ref, sem, sem, partner).wait_recv()

    def sent(ref, sem):
        remote(ref, ref, sem, sem, partner).wait_send()

    small[0].wait()
    wi[pl.ds(512, 16), lane(16 * s + m)] = jnp.broadcast_to(fgain_v[...], (16, 128))

    @pl.loop(1, 16)
    def _(d):
        z_copy(lax.rem(z + d, 16)).start()

    locals_[1].wait()
    locals_[2].wait()

    def win(mm, side):
        return wi.at[:, lane(16 * side + mm)]

    def half_win(mm, up):
        return wi.at[pl.ds(0, 256) if up > 0 else pl.ds(256, 272), lane(16 * s + mm)]

    def b1(up):
        b = win(m, s)
        return remote(b, b, b_s, b1_r.at[up], (s, z, spot(1 if up else 3, 0)))

    def b1_got(up):
        arrived(win(spot(3 if up else 1, 0), s), b1_r.at[up])

    def f1(up):
        b = half_win(spot(3 if up else 1, 0), up)
        return remote(b, b, f_s, f1_r, (s, z, spot(1 if up else 3, 0)))

    def f1_got():
        arrived(win(spot(2, 0), s), f1_r)

    def b2(d, up):
        b = win(spot(d, 0), s)
        return remote(b, b, b_s, b2_r.at[d, up], (s, z, spot(0, 1 if up else 3)))

    def b2_got(d, up):
        arrived(win(spot(d, 3 if up else 1), s), b2_r.at[d, up])

    def f2(d, up):
        b = half_win(spot(d, 3 if up else 1), up)
        return remote(b, b, f_s, f2_r.at[d], (s, z, spot(0, 1 if up else 3)))

    def f2_got(d):
        arrived(win(spot(d, 2), s), f2_r.at[d])

    def pb(d, e):
        b = win(spot(d, e), s)
        return remote(b, b, pb_s, pb_r, partner)

    for up in range(2):
        b1(up).start()
    for up in range(2):
        b2(0, up).start()

    pw = [
        remote(w_up, wu.at[s], pu_s, pu_r, partner),
        remote(w_down, wd.at[s], pd_s, pd_r, partner),
    ]
    pb(0, 0).start()
    for c in pw:
        c.start()

    @pl.loop(1, 16)
    def _(d):
        zo_copy(lax.rem(z + d, 16)).start()

    small[1].wait()
    small[2].wait()
    lens = jnp.broadcast_to(sess_v[...], (32, 32))
    at = lax.broadcasted_iota(jnp.int32, (32, 32), 0)
    of = lax.broadcasted_iota(jnp.int32, (32, 32), 1)
    ends = jnp.sum(jnp.where(of <= at, lens, 0).astype(F32), axis=1, keepdims=True)
    starts = jnp.sum(jnp.where(of < at, lens, 0).astype(F32), axis=1, keepdims=True)
    pos = lax.broadcasted_iota(jnp.int32, (32, 1024), 1).astype(F32)
    limit = jnp.minimum(ends, hist_s[0].astype(F32))
    inside = (pos >= starts) & (pos < limit)
    member[...] = jnp.where(inside, 1.0, 0.0).astype(BF)
    counts = jnp.maximum(limit - starts, 1.0)
    locals_[3].wait()
    pooled_ev[...] = dot(member[...], ev[...])

    home, inner = z // 4, lax.rem(z, 4)
    step = 1 - 2 * ((5 - inner) // 4)
    groups = [home, lax.rem(home + step + 4, 4), lax.rem(home - step + 4, 4), lax.rem(home + 2, 4)]

    def block(g, mm):
        return wa.at[pl.ds(4 * g, 4), s, :, lane(mm)]

    def a1(i, d):
        b = block(groups[i], m)
        return remote(b, b, a1_s, a1_r.at[i], (s, z, spot(d, 0)))

    def a2(i, d, e):
        b = block(groups[i], spot(4 - d, 0))
        return remote(b, b, a2_s, a2_r.at[i], (s, z, spot(0, e)))

    def pa(i, side):
        b = wa.at[pl.ds(4 * groups[i], 4), side]
        return remote(b, b, pa_s, pa_r.at[i], partner)

    def oblock(ff):
        return wo.at[:, s, :, lane(ff)]

    def ao(d):
        b = oblock(first)
        return remote(b, b, ao_s, ao_r, (s, z, spot(d, 0)))

    def po(side):
        b = wo.at[:, side]
        return remote(b, b, po_s, po_r, partner)

    def from_z(i):
        g = groups[i]
        arrived(wa.at[pl.ds(4 * g, 3 if i == 0 else 4), s, :, lane(m)], z_r.at[g])
        for d in (2, 1, 3):
            a1(i, d).start()
        for e in (2, 1, 3):
            a2(i, 0, e).start()

    def from_first(i):
        arrived(wa.at[pl.ds(4 * groups[i], 4), s, :, pl.ds(0, 3 * 128)], a1_r.at[i])
        for e in (2, 1, 3):
            for d in range(1, 4):
                a2(i, d, e).start()

    def from_second(i):
        arrived(wa.at[pl.ds(4 * groups[i], 4), s, :, pl.ds(0, 12 * 128)], a2_r.at[i])
        pa(i, s).start()

    def pass_on(d):
        for up in range(2):
            b2_got(d, up)
            f2(d, up).start()
            pb(d, 3 if up else 1).start()

    def complete(d):
        f2_got(d)
        pb(d, 2).start()

    from_z(0)
    from_z(1)
    for up in range(2):
        b1_got(up)
        f1(up).start()
    pb(3, 0).start()
    pb(1, 0).start()
    from_z(2)
    from_z(3)
    from_first(0)
    from_first(1)
    from_first(2)
    from_first(3)
    for d in (3, 1):
        for up in range(2):
            b2(d, up).start()
    f1_got()
    for up in range(2):
        b2(2, up).start()
    pass_on(0)
    arrived(wo.at[pl.ds(0, 15), s, :, lane(first)], zo_r)
    for d in range(1, 4):
        ao(d).start()
    from_second(0)
    from_second(1)
    from_second(2)
    from_second(3)
    pb(2, 0).start()
    for i in range(2):
        pa(i, 1 - s).wait_recv()

    def tokens_of(lo, i, j):
        at_rows = pl.ds(lo, 256)
        return jnp.concatenate([ev[at_rows, lane(groups[i])], ev[at_rows, lane(groups[j])]], axis=1)

    def weights_of(c, i, j):
        cols = pl.ds(512 * c, 512)
        return jnp.concatenate(
            [wa[pl.ds(4 * groups[k], 4), :, :, cols].reshape(128, 512) for k in (i, j)], axis=0
        )

    for c in range(4):
        w = weights_of(c, 0, 1)
        for r in range(2):
            pre[pl.ds(256 * r, 256), pl.ds(512 * c, 512)] = dot(tokens_of(256 * r, 0, 1), w)

    for i in range(2, 4):
        pa(i, 1 - s).wait_recv()

    small[3].wait()

    def keep(r, parts):
        at_rows = pl.ds(r * 256, 256)
        gs[at_rows, :] = silu(parts(0))
        values = silu(parts(1))
        if r:
            row = r * 256 + lax.broadcasted_iota(jnp.int32, (256, 1), 0)
            values *= jnp.where(row < hist_s[0], 1.0, 0.0).astype(BF)
        vs[at_rows, :] = values
        qs[at_rows, :] = silu(parts(2), 128 ** (-0.5) * 0.5)
        ks[at_rows, :] = silu(parts(3))

    def project(r):
        tokens = ev[pl.ds(r * 256, 256), :]
        keep(r, lambda c: dot(tokens, wa[:, :, :, pl.ds(512 * c, 512)].reshape(512, 512)))

    def project_rest(r):
        tokens = tokens_of(256 * r, 2, 3)
        keep(
            r,
            lambda c: pre[pl.ds(256 * r, 256), pl.ds(512 * c, 512)] + dot(tokens, weights_of(c, 2, 3)),
        )

    diagonal = lax.broadcasted_iota(jnp.int32, (256, 256), 1) <= lax.broadcasted_iota(
        jnp.int32, (256, 256), 0
    )

    def attend(i, heads):
        lo = i * 256
        for h in heads:
            cols = pl.ds(h * 128, 128)
            q = qs[pl.ds(lo, 256), cols]

            def weigh(j):
                u = dot_nt(q, ks[pl.ds(256 * j, 256), cols])
                u = (jnp.where(diagonal, u, 0.0) if j == i else u).astype(BF)
                return u + u * jnp.tanh(u)

            acc = dot(weigh(i), vs[pl.ds(lo, 256), cols])
            for j in range(i):
                acc += dot(weigh(j), vs[pl.ds(256 * j, 256), cols])
            att[pl.ds(lo, 256), cols] = acc

    def gate(i):
        at_rows = pl.ds(i * 256, 256)
        a = att[at_rows, :]
        inv = lax.rsqrt(jnp.mean(a * a, axis=1, keepdims=True) + EPSILON)
        gated[at_rows, :] = (a * inv * gain_v[...] * gs[at_rows, :].astype(F32)).astype(BF)

    def pool(nr, upto):
        mm = member[pl.ds(0, nr), pl.ds(0, upto)]
        pg = dot(mm, gated[pl.ds(0, upto), :])
        hi = pg.astype(BF)
        lo = (pg - hi.astype(F32)).astype(BF)
        both = dot(jnp.concatenate([hi, lo], axis=0), wo[...].reshape(512, 512))
        return pooled_ev[pl.ds(0, nr), :] + both[0:nr] + both[nr : 2 * nr]

    for r in range(2):
        project_rest(r)
    arrived(wo.at[:, s, :, pl.ds(0, 3 * 128)], ao_r)
    po(s).start()
    pass_on(3)
    pass_on(1)
    for i in range(2):
        attend(i, range(4))
        gate(i)
    pass_on(2)
    complete(0)
    po(1 - s).wait_recv()
    early = (pool(16, 512) / counts[0:16])[0:8].astype(BF)
    slot = 4 * first + second
    rows[slot] = early

    def r_copy(to):
        return remote(rows.at[slot], rows.at[slot], r_s, r_r, (s, z, to))

    @pl.loop(1, 16)
    def _(d):
        r_copy(lax.rem(m + d, 16)).start()


    complete(3)
    complete(1)
    project(2)
    complete(2)
    project(3)

    arrived(rows.at[pl.ds(0, 15)], r_r)
    locals_[4].wait()
    locals_[5].wait()
    for c in pw:
        c.wait_recv()
    arrived(wi.at[:, pl.ds(pl.multiple_of((1 - s) * 2048, 128), 2048)], pb_r)

    xs = rows[...].astype(F32).reshape(128, 512).astype(BF)
    acc = jnp.zeros((128, 512), F32)
    sq = jnp.zeros((128, 1), F32)
    for c in range(2):
        cols = pl.ds(c * 2048, 2048)
        h = dot(xs, wi[pl.ds(0, 512), cols])
        hin[:, cols] = h
        g = wi[pl.ds(512, 16), cols].astype(F32)[0:1]
        acc += dot((h * g).astype(BF), wu[c])
        sq += jnp.sum(h * h, axis=1, keepdims=True)
    up = acc * lax.rsqrt(sq * (1.0 / 4096) + EPSILON)
    hidden = jax.nn.gelu(up, approximate=True).astype(BF)

    def chunk(k):
        return pl.ds(k * 1024, 1024)

    def c1(k, d):
        to_first = lax.rem(first + d, 4)
        return remote(
            part.at[pl.ds(4 * to_first, 4), :, chunk(k)], recv.at[d - 1, :, :, chunk(k)],
            c1_s, c1_r.at[k], (s, z, spot(d, 0)),
        )

    def c2(k, e):
        return remote(
            relay.at[e - 1, :, chunk(k)], last.at[e - 1, :, chunk(k)],
            c2_s, c2_r.at[k], (s, z, spot(0, e)),
        )

    for k in range(4):
        p = dot(hidden, wd[k // 2, :, pl.ds((k % 2) * 1024, 1024)])
        part[:, :, chunk(k)] = p.reshape(16, 8, 1024).astype(BF)

        @pl.loop(0, 3)
        def _(i):
            c1(k, 1 + lax.rem(i + 1, 3)).start()


    def relay_chunk(k):
        arrived(recv.at[:, :, :, chunk(k)], c1_r.at[k])
        def total(e):
            gg = lax.rem(second + e, 4)
            t = part[4 * first + gg, :, chunk(k)].astype(F32)
            for d in range(1, 4):
                t += recv[d - 1, gg, :, chunk(k)].astype(F32)
            return t

        for e in range(1, 4):
            relay[e - 1, :, chunk(k)] = total(e).astype(BF)

        @pl.loop(0, 3)
        def _(i):
            c2(k, 1 + lax.rem(i + 1, 3)).start()

        own[:, chunk(k)] = total(0) + hin[pl.ds(pl.multiple_of(slot * 8, 8), 8), chunk(k)]

    def settle():
        sent(wa.at[pl.ds(0, 15), s, :, lane(m)], z_s)
        sent(wo.at[pl.ds(0, 15), s, :, lane(first)], zo_s)
        sent(rows.at[pl.ds(0, 15)], r_s)
        for c in pw:
            c.wait_send()
        sent(wa.at[pl.ds(0, 12), s, :, pl.ds(0, 512)], a1_s)
        sent(wa.at[:, s, :, pl.ds(0, 12 * 128)], a2_s)
        sent(wa.at[:, s], pa_s)
        sent(wo.at[:, s, :, pl.ds(0, 3 * 128)], ao_s)
        po(s).wait_send()
        sent(wi.at[:, pl.ds(0, 10 * 128)], b_s)
        sent(wi.at[:, pl.ds(0, 5 * 128)], f_s)
        sent(wi.at[:, pl.ds(0, 16 * 128)], pb_s)

    attend(2, (0, 1))
    attend(2, (2, 3))
    gate(2)
    relay_chunk(0)
    attend(3, (0, 1))
    relay_chunk(1)
    attend(3, (2, 3))
    relay_chunk(2)
    gate(3)
    pooled_v[...] = (pool(32, 1024) / counts).astype(BF)
    relay_chunk(3)
    pooled_copy = pltpu.make_async_copy(pooled_v, pooled_out, out_s.at[0])
    pooled_copy.start()
    settle()
    for k in range(4):
        t = own[:, chunk(k)]
        arrived(last.at[:, :, chunk(k)], c2_r.at[k])
        for e in range(1, 4):
            t += last[e - 1, :, chunk(k)].astype(F32)
        cross_v[:, chunk(k)] = t.astype(BF)

    def cross_copy(k):
        cols = pl.ds(pl.multiple_of(k * 1024, 1024), 1024)
        return pltpu.make_async_copy(cross_v.at[:, cols], cross_out.at[:, cols], out_s.at[k + 1])

    @pl.loop(0, 4)
    def _(k):
        cross_copy(k).start()

    sent(recv, c1_s)
    sent(relay, c2_s)
    pooled_copy.wait()
    for k in range(4):
        cross_copy(k).wait()


def hand_on(pooled, cross, pooled_out, cross_out):
    pooled_out[...] = pooled[...]
    cross_out[...] = cross[...]


def per_device(events, hist_len, sess_len, w_uvqk, w_out, attn_gain, w_in, ffn_gain, w_up, w_down):
    anywhere = pl.BlockSpec(memory_space=pl.ANY)
    vm = pltpu.VMEM
    outs = (jax.ShapeDtypeStruct((32, 512), BF), jax.ShapeDtypeStruct((8, 4096), BF))
    both = pl.pallas_call(
        kernel,
        out_shape=outs,
        in_specs=[anywhere] * 10,
        out_specs=(anywhere, anywhere),
        scratch_shapes=[
            pltpu.SMEM((1,), jnp.int32),
            vm((1, 32), jnp.int32),
            vm((1, 512), F32),
            vm((1, 128), BF),
            vm((32, 512), BF),
            vm((8, 4096), BF),
            vm((1024, 512), BF),
            vm((16, 2, 16, 2048), BF),
            vm((16, 2, 16, 512), BF),
            vm((528, 4096), BF),
            vm((2, 2048, 512), BF),
            vm((2, 512, 2048), BF),
            vm((1024, 512), BF),
            vm((1024, 512), BF),
            vm((1024, 512), BF),
            vm((1024, 512), BF),
            vm((1024, 512), F32),
            vm((1024, 512), BF),
            vm((32, 1024), BF),
            vm((16, 8, 512), BF),
            vm((128, 4096), F32),
            vm((16, 8, 4096), BF),
            vm((3, 4, 8, 4096), BF),
            vm((3, 8, 4096), BF),
            vm((3, 8, 4096), BF),
            vm((8, 4096), F32),
            vm((512, 2048), F32),
            vm((32, 512), F32),
            DMA((10,)),
            DMA, DMA((4,)), DMA, DMA,
            DMA, DMA((4,)), DMA, DMA,
            DMA, DMA((4,)),
            DMA, DMA((4,)), DMA, DMA,
            DMA, DMA, DMA((2,)), DMA, DMA((4, 2)), DMA((4,)),
            DMA, DMA,
            DMA, DMA, DMA, DMA,
            DMA, DMA,
            DMA, DMA((4,)), DMA, DMA((4,)),
            DMA((5,)),
        ],
        compiler_params=pltpu.CompilerParams(
            collective_id=0, has_side_effects=True, vmem_limit_bytes=60 << 20
        ),
        name="encode_and_mix",
    )(
        events, hist_len, sess_len, w_uvqk.reshape(2, 16, 2048), w_out.reshape(2, 16, 512),
        attn_gain.reshape(1, 512), w_in, ffn_gain, w_up, w_down,
    )
    return pl.pallas_call(hand_on, out_shape=outs, name="hand_on")(*both)


def solution(mesh):
    return jax.shard_map(
        per_device,
        mesh=mesh,
        in_specs=(
            P(("section", "dp", "mp"), None, None),
            P(("section", "dp", "mp")),
            P(("section", "dp", "mp"), None),
            P("dp", None),
            P("dp", None),
            P(),
            P(None, ("section", "mp")),
            P(None, ("section", "mp")),
            P("section", "mp"),
            P("mp", "section"),
        ),
        out_specs=(P(("section", "dp", "mp"), None), P(("section", "dp", "mp"), None)),
        check_vma=False,
    )
```

```python
import jax
import jax.numpy as jnp
from jax import lax
from jax.experimental import pallas as pl
from jax.experimental.pallas import tpu as pltpu
from jax.sharding import PartitionSpec as P

MESH = pl.DeviceIdType.MESH
BF = jnp.bfloat16
F32 = jnp.float32
EPSILON = 1e-06
DMA = pltpu.SemaphoreType.DMA


def dot(a, b):
    return jnp.dot(a, b, preferred_element_type=F32)


def dot_nt(a, b):
    return lax.dot_general(a, b, (((1,), (1,)), ((), ())), preferred_element_type=F32)


def silu(v, scale=None):
    half = (0.5 * v).astype(BF)
    first = half if scale is None else ((0.5 * scale) * v).astype(BF)
    return first + first * jnp.tanh(half)


def kernel(
    events, hist, sess, w_uvqk, w_out, gain, w_in, ffn_gain, w_up, w_down,
    pooled_out, cross_out,
    hist_s, sess_v, gain_v, fgain_v, pooled_v, cross_v,
    ev, wa, wo, wi, wu, wd, qs, ks, vs, gs, att, gated, member, rows, hin, part, recv, relay, last, own,
    pre, pooled_ev, loc, z_s, z_r, zo_s, zo_r, a1_s, a1_r, ao_s, ao_r, a2_s, a2_r, pa_s, pa_r, po_s, po_r,
    b_s, f_s, b1_r, f1_r, b2_r, f2_r, pb_s, pb_r, pu_s, pu_r, pd_s, pd_r, r_s, r_r,
    c1_s, c1_r, c2_s, c2_r, out_s,
):
    s = lax.axis_index("section")
    z = lax.axis_index("dp")
    m = lax.axis_index("mp")
    x = lax.rem(m, 4)
    y = m // 4
    first = (1 - s) * x + s * y
    second = s * x + (1 - s) * y
    partner = (1 - s, z, m)

    barrier = pltpu.get_barrier_semaphore()

    @pl.loop(1, 16)
    def _(d):
        pl.semaphore_signal(barrier, inc=1, device_id=(s, lax.rem(z + d, 16), m), device_id_type=MESH)
        pl.semaphore_signal(barrier, inc=1, device_id=(s, z, lax.rem(m + d, 16)), device_id_type=MESH)

    pl.semaphore_signal(barrier, inc=1, device_id=partner, device_id_type=MESH)

    def spot(d, e):
        xx = lax.rem(x + (1 - s) * d + s * e, 4)
        yy = lax.rem(y + s * d + (1 - s) * e, 4)
        return yy * 4 + xx

    def remote(src, dst, ss, rs, to):
        return pltpu.make_async_remote_copy(
            src_ref=src, dst_ref=dst, send_sem=ss, recv_sem=rs, device_id=to, device_id_type=MESH
        )

    def lane(k):
        return pl.ds(pl.multiple_of(k * 128, 128), 128)

    small = [
        pltpu.make_async_copy(ffn_gain, fgain_v, loc.at[6]),
        pltpu.make_async_copy(sess, sess_v, loc.at[7]),
        pltpu.make_async_copy(hist, hist_s, loc.at[8]),
        pltpu.make_async_copy(gain, gain_v, loc.at[9]),
    ]
    locals_ = [
        pltpu.make_async_copy(w_uvqk.at[s, :, lane(m)], wa.at[z, s, :, lane(m)], loc.at[0]),
        pltpu.make_async_copy(w_out.at[s, :, lane(first)], wo.at[z, s, :, lane(first)], loc.at[1]),
        pltpu.make_async_copy(w_in, wi.at[pl.ds(0, 512), lane(16 * s + m)], loc.at[3]),
        pltpu.make_async_copy(events.at[0], ev, loc.at[2]),
        pltpu.make_async_copy(w_up, wu.at[s], loc.at[4]),
        pltpu.make_async_copy(w_down, wd.at[s], loc.at[5]),
    ]
    for c in locals_[:2] + small + locals_[2:]:
        c.start()

    pl.semaphore_wait(barrier, 31)
    locals_[0].wait()

    def z_copy(to_z):
        b = wa.at[z, s, :, lane(m)]
        return remote(b, b, z_s, z_r.at[z // 4], (s, to_z, m))

    def zo_copy(to_z):
        b = wo.at[z, s, :, lane(first)]
        return remote(b, b, zo_s, zo_r, (s, to_z, m))

    def arrived(ref, sem):
        remote(ref, ref, sem, sem, partner).wait_recv()

    def sent(ref, sem):
        remote(ref, ref, sem, sem, partner).wait_send()

    small[0].wait()
    wi[pl.ds(512, 16), lane(16 * s + m)] = jnp.broadcast_to(fgain_v[...], (16, 128))

    @pl.loop(1, 16)
    def _(d):
        z_copy(lax.rem(z + d, 16)).start()

    locals_[1].wait()
    locals_[2].wait()

    def win(mm, side):
        return wi.at[:, lane(16 * side + mm)]

    def half_win(mm, up):
        return wi.at[pl.ds(0, 256) if up > 0 else pl.ds(256, 272), lane(16 * s + mm)]

    def b1(up):
        b = win(m, s)
        return remote(b, b, b_s, b1_r.at[up], (s, z, spot(1 if up else 3, 0)))

    def b1_got(up):
        arrived(win(spot(3 if up else 1, 0), s), b1_r.at[up])

    def f1(up):
        b = half_win(spot(3 if up else 1, 0), up)
        return remote(b, b, f_s, f1_r, (s, z, spot(1 if up else 3, 0)))

    def f1_got():
        arrived(win(spot(2, 0), s), f1_r)

    def b2(d, up):
        b = win(spot(d, 0), s)
        return remote(b, b, b_s, b2_r.at[d, up], (s, z, spot(0, 1 if up else 3)))

    def b2_got(d, up):
        arrived(win(spot(d, 3 if up else 1), s), b2_r.at[d, up])

    def f2(d, up):
        b = half_win(spot(d, 3 if up else 1), up)
        return remote(b, b, f_s, f2_r.at[d], (s, z, spot(0, 1 if up else 3)))

    def f2_got(d):
        arrived(win(spot(d, 2), s), f2_r.at[d])

    def pb(d, e):
        b = win(spot(d, e), s)
        return remote(b, b, pb_s, pb_r, partner)

    for up in range(2):
        b1(up).start()
    for up in range(2):
        b2(0, up).start()

    pw = [
        remote(w_up, wu.at[s], pu_s, pu_r, partner),
        remote(w_down, wd.at[s], pd_s, pd_r, partner),
    ]
    pb(0, 0).start()
    for c in pw:
        c.start()

    @pl.loop(1, 16)
    def _(d):
        zo_copy(lax.rem(z + d, 16)).start()

    small[1].wait()
    small[2].wait()
    lens = jnp.broadcast_to(sess_v[...], (32, 32))
    at = lax.broadcasted_iota(jnp.int32, (32, 32), 0)
    of = lax.broadcasted_iota(jnp.int32, (32, 32), 1)
    ends = jnp.sum(jnp.where(of <= at, lens, 0).astype(F32), axis=1, keepdims=True)
    starts = jnp.sum(jnp.where(of < at, lens, 0).astype(F32), axis=1, keepdims=True)
    pos = lax.broadcasted_iota(jnp.int32, (32, 1024), 1).astype(F32)
    limit = jnp.minimum(ends, hist_s[0].astype(F32))
    inside = (pos >= starts) & (pos < limit)
    member[...] = jnp.where(inside, 1.0, 0.0).astype(BF)
    counts = jnp.maximum(limit - starts, 1.0)
    locals_[3].wait()
    pooled_ev[...] = dot(member[...], ev[...])

    home, inner = z // 4, lax.rem(z, 4)
    step = 1 - 2 * ((5 - inner) // 4)
    groups = [home, lax.rem(home + step + 4, 4), lax.rem(home - step + 4, 4), lax.rem(home + 2, 4)]

    def block(g, mm):
        return wa.at[pl.ds(4 * g, 4), s, :, lane(mm)]

    def a1(i, d):
        b = block(groups[i], m)
        return remote(b, b, a1_s, a1_r.at[i], (s, z, spot(d, 0)))

    def a2(i, d, e):
        b = block(groups[i], spot(4 - d, 0))
        return remote(b, b, a2_s, a2_r.at[i], (s, z, spot(0, e)))

    def pa(i, side):
        b = wa.at[pl.ds(4 * groups[i], 4), side]
        return remote(b, b, pa_s, pa_r.at[i], partner)

    def oblock(ff):
        return wo.at[:, s, :, lane(ff)]

    def ao(d):
        b = oblock(first)
        return remote(b, b, ao_s, ao_r, (s, z, spot(d, 0)))

    def po(side):
        b = wo.at[:, side]
        return remote(b, b, po_s, po_r, partner)

    def from_z(i):
        g = groups[i]
        arrived(wa.at[pl.ds(4 * g, 3 if i == 0 else 4), s, :, lane(m)], z_r.at[g])
        for d in (2, 1, 3):
            a1(i, d).start()
        for e in (2, 1, 3):
            a2(i, 0, e).start()

    def from_first(i):
        arrived(wa.at[pl.ds(4 * groups[i], 4), s, :, pl.ds(0, 3 * 128)], a1_r.at[i])
        for e in (2, 1, 3):
            for d in range(1, 4):
                a2(i, d, e).start()

    def from_second(i):
        arrived(wa.at[pl.ds(4 * groups[i], 4), s, :, pl.ds(0, 12 * 128)], a2_r.at[i])
        pa(i, s).start()

    def pass_on(d):
        for up in range(2):
            b2_got(d, up)
            f2(d, up).start()
            pb(d, 3 if up else 1).start()

    def complete(d):
        f2_got(d)
        pb(d, 2).start()

    from_z(0)
    from_z(1)
    for up in range(2):
        b1_got(up)
        f1(up).start()
    pb(3, 0).start()
    pb(1, 0).start()
    from_z(2)
    from_z(3)
    from_first(0)
    from_first(1)
    from_first(2)
    from_first(3)
    for d in (3, 1):
        for up in range(2):
            b2(d, up).start()
    f1_got()
    for up in range(2):
        b2(2, up).start()
    pass_on(0)
    arrived(wo.at[pl.ds(0, 15), s, :, lane(first)], zo_r)
    for d in range(1, 4):
        ao(d).start()
    from_second(0)
    from_second(1)
    from_second(2)
    from_second(3)
    pb(2, 0).start()
    for i in range(2):
        pa(i, 1 - s).wait_recv()

    def tokens_of(lo, i, j):
        at_rows = pl.ds(lo, 256)
        return jnp.concatenate([ev[at_rows, lane(groups[i])], ev[at_rows, lane(groups[j])]], axis=1)

    def weights_of(c, i, j):
        cols = pl.ds(512 * c, 512)
        return jnp.concatenate(
            [wa[pl.ds(4 * groups[k], 4), :, :, cols].reshape(128, 512) for k in (i, j)], axis=0
        )

    for c in range(4):
        w = weights_of(c, 0, 1)
        for r in range(2):
            pre[pl.ds(256 * r, 256), pl.ds(512 * c, 512)] = dot(tokens_of(256 * r, 0, 1), w)

    for i in range(2, 4):
        pa(i, 1 - s).wait_recv()

    small[3].wait()

    def keep(r, parts):
        at_rows = pl.ds(r * 256, 256)
        gs[at_rows, :] = silu(parts(0))
        values = silu(parts(1))
        if r:
            row = r * 256 + lax.broadcasted_iota(jnp.int32, (256, 1), 0)
            values *= jnp.where(row < hist_s[0], 1.0, 0.0).astype(BF)
        vs[at_rows, :] = values
        qs[at_rows, :] = silu(parts(2), 128 ** (-0.5) * 0.5)
        ks[at_rows, :] = silu(parts(3))

    def project(r):
        tokens = ev[pl.ds(r * 256, 256), :]
        keep(r, lambda c: dot(tokens, wa[:, :, :, pl.ds(512 * c, 512)].reshape(512, 512)))

    def project_rest(r):
        tokens = tokens_of(256 * r, 2, 3)
        keep(
            r,
            lambda c: pre[pl.ds(256 * r, 256), pl.ds(512 * c, 512)] + dot(tokens, weights_of(c, 2, 3)),
        )

    diagonal = lax.broadcasted_iota(jnp.int32, (256, 256), 1) <= lax.broadcasted_iota(
        jnp.int32, (256, 256), 0
    )

    def attend(i, heads):
        lo = i * 256
        for h in heads:
            cols = pl.ds(h * 128, 128)
            q = qs[pl.ds(lo, 256), cols]

            def weigh(j):
                u = dot_nt(q, ks[pl.ds(256 * j, 256), cols])
                u = (jnp.where(diagonal, u, 0.0) if j == i else u).astype(BF)
                return u + u * jnp.tanh(u)

            acc = dot(weigh(i), vs[pl.ds(lo, 256), cols])
            for j in range(i):
                acc += dot(weigh(j), vs[pl.ds(256 * j, 256), cols])
            att[pl.ds(lo, 256), cols] = acc

    def gate(i):
        at_rows = pl.ds(i * 256, 256)
        a = att[at_rows, :]
        inv = lax.rsqrt(jnp.mean(a * a, axis=1, keepdims=True) + EPSILON)
        gated[at_rows, :] = (a * inv * gain_v[...] * gs[at_rows, :].astype(F32)).astype(BF)

    def pool(nr, upto):
        mm = member[pl.ds(0, nr), pl.ds(0, upto)]
        pg = dot(mm, gated[pl.ds(0, upto), :])
        hi = pg.astype(BF)
        lo = (pg - hi.astype(F32)).astype(BF)
        both = dot(jnp.concatenate([hi, lo], axis=0), wo[...].reshape(512, 512))
        return pooled_ev[pl.ds(0, nr), :] + both[0:nr] + both[nr : 2 * nr]

    for r in range(2):
        project_rest(r)
    arrived(wo.at[:, s, :, pl.ds(0, 3 * 128)], ao_r)
    po(s).start()
    pass_on(3)
    attend(0, range(4))
    gate(0)
    pass_on(1)
    pass_on(2)
    complete(0)
    attend(1, range(4))
    gate(1)
    po(1 - s).wait_recv()
    early = (pool(16, 512) / counts[0:16])[0:8].astype(BF)
    slot = 4 * first + second
    rows[slot] = early

    def r_copy(to):
        return remote(rows.at[slot], rows.at[slot], r_s, r_r, (s, z, to))

    @pl.loop(1, 16)
    def _(d):
        r_copy(lax.rem(m + d, 16)).start()


    complete(3)
    complete(1)
    project(2)
    complete(2)
    project(3)

    arrived(rows.at[pl.ds(0, 15)], r_r)
    locals_[4].wait()
    locals_[5].wait()
    for c in pw:
        c.wait_recv()
    arrived(wi.at[:, pl.ds(pl.multiple_of((1 - s) * 2048, 128), 2048)], pb_r)

    xs = rows[...].astype(F32).reshape(128, 512).astype(BF)
    acc = jnp.zeros((128, 512), F32)
    sq = jnp.zeros((128, 1), F32)
    for c in range(2):
        cols = pl.ds(c * 2048, 2048)
        h = dot(xs, wi[pl.ds(0, 512), cols])
        hin[:, cols] = h
        g = wi[pl.ds(512, 16), cols].astype(F32)[0:1]
        acc += dot((h * g).astype(BF), wu[c])
        sq += jnp.sum(h * h, axis=1, keepdims=True)
    up = acc * lax.rsqrt(sq * (1.0 / 4096) + EPSILON)
    hidden = jax.nn.gelu(up, approximate=True).astype(BF)

    def chunk(k):
        return pl.ds(k * 1024, 1024)

    def c1(k, d):
        to_first = lax.rem(first + d, 4)
        return remote(
            part.at[pl.ds(4 * to_first, 4), :, chunk(k)], recv.at[d - 1, :, :, chunk(k)],
            c1_s, c1_r.at[k], (s, z, spot(d, 0)),
        )

    def c2(k, e):
        return remote(
            relay.at[e - 1, :, chunk(k)], last.at[e - 1, :, chunk(k)],
            c2_s, c2_r.at[k], (s, z, spot(0, e)),
        )

    for k in range(4):
        p = dot(hidden, wd[k // 2, :, pl.ds((k % 2) * 1024, 1024)])
        part[:, :, chunk(k)] = p.reshape(16, 8, 1024).astype(BF)

        @pl.loop(0, 3)
        def _(i):
            c1(k, 1 + lax.rem(i + 1, 3)).start()


    def relay_chunk(k):
        arrived(recv.at[:, :, :, chunk(k)], c1_r.at[k])
        def total(e):
            gg = lax.rem(second + e, 4)
            t = part[4 * first + gg, :, chunk(k)].astype(F32)
            for d in range(1, 4):
                t += recv[d - 1, gg, :, chunk(k)].astype(F32)
            return t

        for e in range(1, 4):
            relay[e - 1, :, chunk(k)] = total(e).astype(BF)

        @pl.loop(0, 3)
        def _(i):
            c2(k, 1 + lax.rem(i + 1, 3)).start()

        own[:, chunk(k)] = total(0) + hin[pl.ds(pl.multiple_of(slot * 8, 8), 8), chunk(k)]

    def settle():
        sent(wa.at[pl.ds(0, 15), s, :, lane(m)], z_s)
        sent(wo.at[pl.ds(0, 15), s, :, lane(first)], zo_s)
        sent(rows.at[pl.ds(0, 15)], r_s)
        for c in pw:
            c.wait_send()
        sent(wa.at[pl.ds(0, 12), s, :, pl.ds(0, 512)], a1_s)
        sent(wa.at[:, s, :, pl.ds(0, 12 * 128)], a2_s)
        sent(wa.at[:, s], pa_s)
        sent(wo.at[:, s, :, pl.ds(0, 3 * 128)], ao_s)
        po(s).wait_send()
        sent(wi.at[:, pl.ds(0, 10 * 128)], b_s)
        sent(wi.at[:, pl.ds(0, 5 * 128)], f_s)
        sent(wi.at[:, pl.ds(0, 16 * 128)], pb_s)

    attend(2, (0, 1))
    attend(2, (2, 3))
    gate(2)
    relay_chunk(0)
    attend(3, (0, 1))
    relay_chunk(1)
    attend(3, (2, 3))
    relay_chunk(2)
    gate(3)
    pooled_v[...] = (pool(32, 1024) / counts).astype(BF)
    relay_chunk(3)
    pooled_copy = pltpu.make_async_copy(pooled_v, pooled_out, out_s.at[0])
    pooled_copy.start()
    settle()
    for k in range(4):
        t = own[:, chunk(k)]
        arrived(last.at[:, :, chunk(k)], c2_r.at[k])
        for e in range(1, 4):
            t += last[e - 1, :, chunk(k)].astype(F32)
        cross_v[:, chunk(k)] = t.astype(BF)

    def cross_copy(k):
        cols = pl.ds(pl.multiple_of(k * 1024, 1024), 1024)
        return pltpu.make_async_copy(cross_v.at[:, cols], cross_out.at[:, cols], out_s.at[k + 1])

    @pl.loop(0, 4)
    def _(k):
        cross_copy(k).start()

    sent(recv, c1_s)
    sent(relay, c2_s)
    pooled_copy.wait()
    for k in range(4):
        cross_copy(k).wait()


def hand_on(pooled, cross, pooled_out, cross_out):
    pooled_out[...] = pooled[...]
    cross_out[...] = cross[...]


def per_device(events, hist_len, sess_len, w_uvqk, w_out, attn_gain, w_in, ffn_gain, w_up, w_down):
    anywhere = pl.BlockSpec(memory_space=pl.ANY)
    vm = pltpu.VMEM
    outs = (jax.ShapeDtypeStruct((32, 512), BF), jax.ShapeDtypeStruct((8, 4096), BF))
    both = pl.pallas_call(
        kernel,
        out_shape=outs,
        in_specs=[anywhere] * 10,
        out_specs=(anywhere, anywhere),
        scratch_shapes=[
            pltpu.SMEM((1,), jnp.int32),
            vm((1, 32), jnp.int32),
            vm((1, 512), F32),
            vm((1, 128), BF),
            vm((32, 512), BF),
            vm((8, 4096), BF),
            vm((1024, 512), BF),
            vm((16, 2, 16, 2048), BF),
            vm((16, 2, 16, 512), BF),
            vm((528, 4096), BF),
            vm((2, 2048, 512), BF),
            vm((2, 512, 2048), BF),
            vm((1024, 512), BF),
            vm((1024, 512), BF),
            vm((1024, 512), BF),
            vm((1024, 512), BF),
            vm((1024, 512), F32),
            vm((1024, 512), BF),
            vm((32, 1024), BF),
            vm((16, 8, 512), BF),
            vm((128, 4096), F32),
            vm((16, 8, 4096), BF),
            vm((3, 4, 8, 4096), BF),
            vm((3, 8, 4096), BF),
            vm((3, 8, 4096), BF),
            vm((8, 4096), F32),
            vm((512, 2048), F32),
            vm((32, 512), F32),
            DMA((10,)),
            DMA, DMA((4,)), DMA, DMA,
            DMA, DMA((4,)), DMA, DMA,
            DMA, DMA((4,)),
            DMA, DMA((4,)), DMA, DMA,
            DMA, DMA, DMA((2,)), DMA, DMA((4, 2)), DMA((4,)),
            DMA, DMA,
            DMA, DMA, DMA, DMA,
            DMA, DMA,
            DMA, DMA((4,)), DMA, DMA((4,)),
            DMA((5,)),
        ],
        compiler_params=pltpu.CompilerParams(
            collective_id=0, has_side_effects=True, vmem_limit_bytes=60 << 20
        ),
        name="encode_and_mix",
    )(
        events, hist_len, sess_len, w_uvqk.reshape(2, 16, 2048), w_out.reshape(2, 16, 512),
        attn_gain.reshape(1, 512), w_in, ffn_gain, w_up, w_down,
    )
    return pl.pallas_call(hand_on, out_shape=outs, name="hand_on")(*both)


def solution(mesh):
    return jax.shard_map(
        per_device,
        mesh=mesh,
        in_specs=(
            P(("section", "dp", "mp"), None, None),
            P(("section", "dp", "mp")),
            P(("section", "dp", "mp"), None),
            P("dp", None),
            P("dp", None),
            P(),
            P(None, ("section", "mp")),
            P(None, ("section", "mp")),
            P("section", "mp"),
            P("mp", "section"),
        ),
        out_specs=(P(("section", "dp", "mp"), None), P(("section", "dp", "mp"), None)),
        check_vma=False,
    )
```
